128 devices in a mesh: grp: 4 (over z), wide: 32 (over y, x, core).
Axes of the slice: x: 4, y: 4, z: 4, core: 2. Of those that a mesh axis runs over, the one named last changes fastest.
Arguments:
- visibilities: bfloat16 [2, 8, 2048, 4096], P(None, None, 'wide', 'grp'), may hold values from -6 to 6
- filters: bfloat16 [4096, 64, 2048], P(('grp', 'wide')), may hold values from -0.125 to 0.125
- counts: int32 [4096], replicated, may hold values from 128 to 2048, as said below
- m_of_slot: int32 [4096], replicated, may hold values from 0 to 4095, each once
- band_of_block: int32 [4096, 8], replicated, may hold values from 0 to 1023
Outputs:
- kl_coeffs: bfloat16 [4096, 2, 8, 64], P(('grp', 'wide'))
- band_power: float32 [8, 1024], P(None, ('grp', 'wide'))
The draws below stay inside these ranges and needn't reach their ends.
Inputs may be any that keep to these rules, and one draw needn't show every extreme that they name: Mode m uses its first counts[m] baselines; both ends of the range are taken in every draw. `m_of_slot`: each m mode stands in exactly one slot.
All inputs are finite; a program needn't handle non-finite values.
Results may differ from the reference program's by a relative error of at most 0.0055.
Values may be sent and summed in bfloat16 or wider, within the bound.
No kernel may reach another device: no remote copies, remote signals or barrier semaphores. Data moves between devices by JAX's collectives and lax.ppermute only.
A program may use at most 128 MiB of HBM per device.

```python
import math
import jax
import jax.numpy as jnp
from jax import lax

CH = 8
NB = 2048
NT = 4096
KL = 64
KB = 8
NBAND = 1024
NKB = 8


def draw_counts(key, part):
    modes = jnp.arange(NT, dtype=jnp.int32)
    lowest = NB // 16
    highest = NB - 7 * NB // 8 * modes // NT
    values = jax.random.randint(key, (NT,), lowest, highest + 1, dtype=jnp.int32)
    values = values.at[0].set(NB)
    values = values.at[NT - 1].set(lowest)
    return values


def place_ends(array, own_key, low, largest):
    longest = array.shape.index(max(array.shape))
    spots = []
    for shift in (0, 1):
        where = [jax.random.randint(jax.random.fold_in(own_key, axis), (), 0, length) for axis, length in enumerate(array.shape)]
        where[longest] = (where[longest] + shift) % array.shape[longest]
        spots.append(tuple(where))
    return array.at[spots[0]].set(low).at[spots[1]].set(largest)


def steps_of(key, shape, pieces, low, largest):
    gain, own = 1.0, jax.random.fold_in(key, 6)
    for position, shards_of in pieces:
        draws = jnp.exp(jax.random.uniform(jax.random.fold_in(own, position), (shards_of,), jnp.float32, low / len(pieces), largest / len(pieces)))
        gain = gain * jnp.repeat(draws, shape[position] // shards_of).reshape([-1 if axis == position else 1 for axis in range(len(shape))])
    return gain


def centred(rng, extent, deviation, reach, split=(), kind=jnp.bfloat16):
    factor_of = steps_of(rng, extent, split, -0.22, 0.18) if split else 1.0
    drawn = jax.random.normal(rng, extent, jnp.float32) * deviation * factor_of
    return jnp.minimum(jnp.maximum(drawn, -reach), reach).astype(kind)


def setup_inputs(seed: int = 0) -> dict:
    arg_keys = jax.random.split(jax.random.key(seed), 6)
    return {
        "visibilities": centred(arg_keys[0], (2, CH, NB, NT), 1.0, 6.0, ((2, 32), (3, 4))),
        "filters": centred(arg_keys[1], (NT, KL, NB), NB ** -0.5, 0.125, ((0, 128),)),
        "counts": draw_counts(jax.random.fold_in(arg_keys[5], 71), 0),
        "m_of_slot": jax.random.permutation(arg_keys[3], NT).astype(jnp.int32),
        "band_of_block": place_ends(jax.random.randint(arg_keys[4], (NT, NKB), 0, NBAND), jax.random.fold_in(arg_keys[4], 1), 0, NBAND - 1).astype(jnp.int32),
    }


def table_block(columns):
    times = jnp.arange(NT, dtype=jnp.int32)
    index = (times[:, None] * columns[None, :] % NT).astype(jnp.int32)
    angles = index.astype(jnp.float32) * (2.0 * math.pi / NT)
    return (jnp.cos(angles).astype(jnp.bfloat16), jnp.sin(angles).astype(jnp.bfloat16))

def reference(visibilities, filters, counts, m_of_slot, band_of_block):
    highest = lax.Precision.HIGHEST
    scale_dft = 1.0 / math.sqrt(NT)
    real_part = visibilities[0].reshape(CH * NB, NT).astype(jnp.float32)
    imag_part = visibilities[1].reshape(CH * NB, NT).astype(jnp.float32)
    mode_block = min(512, NT)

    def transform(columns):
        cos_table, sin_table = table_block(columns)
        cos_full = cos_table.astype(jnp.float32)
        sin_full = sin_table.astype(jnp.float32)
        spec_re = (jnp.dot(real_part, cos_full, precision=highest) + jnp.dot(imag_part, sin_full, precision=highest)) * scale_dft
        spec_im = (jnp.dot(imag_part, cos_full, precision=highest) - jnp.dot(real_part, sin_full, precision=highest)) * scale_dft
        return jnp.stack([spec_re, spec_im]).astype(jnp.bfloat16)
    blocks = lax.map(transform, m_of_slot.reshape(NT // mode_block, mode_block))
    spectrum = blocks.transpose(0, 3, 1, 2).reshape(NT, 2, CH, NB)
    slot_block = min(128, NT)
    slot_counts = counts[m_of_slot]

    def apply_filter(items):
        filter_rows, spec_rows, count_rows = items
        active = jnp.arange(NB, dtype=jnp.int32)[None, :] < count_rows[:, None]
        masked = jnp.where(active[:, None, None, :], spec_rows.astype(jnp.float32), 0.0)
        return jnp.einsum('sxcb,skb->sxck', masked, filter_rows.astype(jnp.float32), precision=highest)
    coeffs = lax.map(apply_filter, (filters.reshape(NT // slot_block, slot_block, KL, NB), spectrum.reshape(NT // slot_block, slot_block, 2, CH, NB), slot_counts.reshape(NT // slot_block, slot_block))).reshape(NT, 2, CH, KL)
    kl_coeffs = coeffs.astype(jnp.bfloat16)
    power = coeffs[:, 0] * coeffs[:, 0] + coeffs[:, 1] * coeffs[:, 1]
    block_power = power.reshape(NT, CH, NKB, KB).sum(axis=-1)
    band_ids = band_of_block[m_of_slot].reshape(-1)
    flat = block_power.transpose(0, 2, 1).reshape(NT * NKB, CH)
    sums = jax.ops.segment_sum(flat, band_ids, num_segments=NBAND)
    band_power = sums.T * (NBAND / (NT * KL))
    return (kl_coeffs, band_power)
```

```python
import math

import jax
import jax.numpy as jnp
import numpy as np
from jax import lax
from jax.experimental import pallas as pl
from jax.experimental.pallas import tpu as pltpu
from jax.sharding import Mesh
from jax.sharding import PartitionSpec as P

CH = 8
NB = 2048
NT = 4096
KL = 64
KB = 8
NBAND = 1024
NKB = 8

DEVS = 128
SLOTS = NT // DEVS
LANES = 128
N2 = NT // LANES
ALL = ("grp", "yx", "core")
F32 = jnp.float32
BF16 = jnp.bfloat16
NT_DIMS = (((1,), (1,)), ((), ()))


def inner_matrix():
    n = np.arange(LANES)
    angle = 2.0 * np.pi * ((n[:, None] * n[None, :]) % LANES) / LANES
    c, s = np.cos(angle) / math.sqrt(NT), np.sin(angle) / math.sqrt(NT)
    re = np.concatenate([c, s], axis=1)
    im = np.concatenate([-s, c], axis=1)
    return np.stack([re, im], axis=1).reshape(2 * LANES, 2 * LANES)


def twiddles():
    m2 = np.arange(N2)[:, None]
    t1 = np.arange(LANES)[None, :]
    angle = 2.0 * np.pi * ((m2 * t1) % NT) / NT
    return np.cos(angle).astype(np.float32), np.sin(angle).astype(np.float32)


def cmul_const(re, im, angle):
    c, s = math.cos(angle), math.sin(angle)
    return re * c + im * s, im * c - re * s


def dft4(x):
    (ar, ai), (br, bi), (cr, ci), (dr, di) = x
    pr, pi, qr, qi = ar + cr, ai + ci, ar - cr, ai - ci
    rr, ri, sr, si = br + dr, bi + di, br - dr, bi - di
    return [(pr + rr, pi + ri), (qr + si, qi - sr), (pr - rr, pi - ri), (qr - si, qi + sr)]


def dft8(x):
    even = dft4([x[0], x[2], x[4], x[6]])
    odd = dft4([x[1], x[3], x[5], x[7]])
    h = math.sqrt(0.5)
    o0 = odd[0]
    o1 = ((odd[1][0] + odd[1][1]) * h, (odd[1][1] - odd[1][0]) * h)
    o2 = (odd[2][1], -odd[2][0])
    o3 = ((odd[3][1] - odd[3][0]) * h, (odd[3][0] + odd[3][1]) * -h)
    lo, hi = [], []
    for (er, ei), (pr, pi) in zip(even, [o0, o1, o2, o3]):
        lo.append((er + pr, ei + pi))
        hi.append((er - pr, ei - pi))
    return lo + hi


def transform_kernel(rows_ref, x_ref, w_ref, twc_ref, tws_ref, o_ref, mid, d_ref, spec, picked):
    def outer(rg, carry):
        core = rg // 4
        r0 = pl.multiple_of((rg % 4) * 16, 16)
        for j in range(8):
            cols = slice(j * LANES, (j + 1) * LANES)
            x = [
                tuple(x_ref[2 * g + core, p, pl.ds(r0, 16), cols].astype(F32) for p in range(2))
                for g in range(4)
            ]
            for q, (re, im) in enumerate(dft4(x)):
                if j * q:
                    re, im = cmul_const(re, im, 2.0 * math.pi * j * q / N2)
                mid[q, j, 0] = re
                mid[q, j, 1] = im
        out0 = pl.multiple_of(rg * 16, 16)
        for q in range(4):
            for half in range(2):
                rows = slice(half * 8, half * 8 + 8)
                y = dft8([(mid[q, j, 0, rows], mid[q, j, 1, rows]) for j in range(8)])
                for p, (re, im) in enumerate(y):
                    m2 = q + 4 * p
                    c = twc_ref[m2 : m2 + 1, :]
                    s = tws_ref[m2 : m2 + 1, :]
                    mid[q, p, 0, rows] = re * c + im * s
                    mid[q, p, 1, rows] = im * c - re * s
            for p in range(8):
                for part in range(2):
                    d_ref[q + 4 * p, pl.ds(out0, 16), part * LANES : (part + 1) * LANES] = mid[
                        q, p, part
                    ].astype(BF16)
        return carry

    lax.fori_loop(0, 8, outer, 0)

    def inner(m2, carry):
        spec[pl.ds(pl.multiple_of(m2 * 256, 256), 256), :] = lax.dot_general(
            w_ref[...], d_ref[m2], NT_DIMS, preferred_element_type=F32
        )
        return carry

    lax.fori_loop(0, N2, inner, 0, unroll=2)

    def pick(step, carry):
        base = step * 32
        for u in range(32):
            row = pl.multiple_of(rows_ref[base + u], 2)
            picked[pl.ds(pl.multiple_of((base + u) * 2, 2), 2), :] = spec[pl.ds(row, 2), :]
        return carry

    lax.fori_loop(0, NT // 32, pick, 0)

    def narrow(step, carry):
        where = pl.ds(pl.multiple_of(step * 256, 256), 256)
        o_ref[where, :] = picked[where, :].astype(BF16)
        return carry

    lax.fori_loop(0, 2 * NT // 256, narrow, 0, unroll=2)


def mask_kernel(counts_ref, f_ref, o_ref):
    step = pl.program_id(0)
    column = lax.broadcasted_iota(jnp.int32, (KL, NB), 1)
    for s in range(8):
        rows = slice(s * KL, (s + 1) * KL)
        keep = column < counts_ref[step * 8 + s]
        o_ref[rows, :] = jnp.where(keep, f_ref[rows, :], jnp.zeros((), BF16))


def split3(x):
    a = x.astype(BF16)
    r = x - a.astype(F32)
    b = r.astype(BF16)
    return a, b, (r - b.astype(F32)).astype(BF16)


def iota(shape, axis):
    return lax.broadcasted_iota(jnp.int32, shape, axis)


def filter_kernel(x_ref, f_ref, col_ref, row_ref, kl_ref, band_ref, lhs, rhs):
    step = pl.program_id(0)
    r0 = pl.multiple_of(step * 16, 16)
    for k in range(16):
        lhs[:, k * LANES : (k + 1) * LANES] = x_ref[:, k, :, pl.ds(r0, 16), :].reshape(128, LANES)
    acc = lax.dot_general(lhs[...], f_ref[...], NT_DIMS, preferred_element_type=F32)
    own = ((iota((128, 512), 0) // 2) % 8) == (iota((128, 512), 1) // KL)
    acc = jnp.where(own, acc, 0.0)
    pairs = acc[:, 0:128] + acc[:, 128:256] + acc[:, 256:384] + acc[:, 384:512]
    mine = (pairs[:, :KL] + pairs[:, KL:]).astype(BF16)
    to, frm = iota((128, 128), 0), iota((128, 128), 1)
    order = jnp.where(frm == (to % 8) * 16 + to // 8, 1.0, 0.0).astype(BF16)
    kl_ref[...] = jnp.dot(order, mine, preferred_element_type=F32).astype(BF16)
    power = (acc * acc).reshape(8, 16, 512).sum(axis=1)
    spread = jnp.broadcast_to(power[:, None, :], (8, 8, 512)).reshape(64, 512)
    blocks = jnp.where(iota((64, 512), 1) // KB == iota((64, 512), 0), 1.0, 0.0).astype(BF16)
    table = sum(
        lax.dot_general(blocks, part, NT_DIMS, preferred_element_type=F32) for part in split3(spread)
    )
    band = col_ref[...]
    low = iota((64, 64), 1) % 8
    table = jnp.where((band[:, :64] % 8) == low, table, 0.0)
    rhs[pl.ds(pl.multiple_of(step * 64, 64), 64), :] = jnp.concatenate(
        [table, jnp.zeros((64, 64), F32)], axis=1
    )

    @pl.when(step == 3)
    def _():
        high = row_ref[0:1, :] // 8
        hot = jnp.where(iota((128, 256), 0) == high, 1.0, 0.0).astype(BF16)
        total = sum(jnp.dot(hot, part, preferred_element_type=F32) for part in split3(rhs[...]))
        band_ref[...] = total


def body(visibilities, filters, counts, m_of_slot, band_of_block):
    place = lax.axis_index(ALL)
    mine = lax.dynamic_slice_in_dim(m_of_slot, place * SLOTS, SLOTS)
    slot_counts = counts[mine]
    band = band_of_block[mine].reshape(SLOTS * NKB)
    band_col = jnp.broadcast_to(band[:, None], (SLOTS * NKB, 128))
    band_row = jnp.broadcast_to(band[None, :], (8, SLOTS * NKB))
    rows = (m_of_slot % N2) * (2 * LANES) + (m_of_slot // N2) * 2

    sent = visibilities.transpose(1, 0, 2, 3)
    local = lax.all_to_all(sent, ("grp", "core"), 0, 0, tiled=True)

    masked = pl.pallas_call(
        mask_kernel,
        out_shape=jax.ShapeDtypeStruct((SLOTS * KL, NB), BF16),
        grid_spec=pltpu.PrefetchScalarGridSpec(
            num_scalar_prefetch=1,
            grid=(4,),
            in_specs=[pl.BlockSpec((8 * KL, NB), lambda i, c: (i, 0))],
            out_specs=pl.BlockSpec((8 * KL, NB), lambda i, c: (i, 0)),
        ),
        name="mask",
    )(slot_counts, filters.reshape(SLOTS * KL, NB))

    tw_cos, tw_sin = twiddles()
    spectrum = pl.pallas_call(
        transform_kernel,
        out_shape=jax.ShapeDtypeStruct((2 * NT, LANES), BF16),
        grid_spec=pltpu.PrefetchScalarGridSpec(
            num_scalar_prefetch=1,
            grid=(1,),
            in_specs=[
                pl.BlockSpec((8, 2, 64, 1024), lambda i, r: (0, 0, 0, 0)),
                pl.BlockSpec((256, 256), lambda i, r: (0, 0)),
                pl.BlockSpec((N2, LANES), lambda i, r: (0, 0)),
                pl.BlockSpec((N2, LANES), lambda i, r: (0, 0)),
            ],
            out_specs=pl.BlockSpec((2 * NT, LANES), lambda i, r: (0, 0)),
            scratch_shapes=[
                pltpu.VMEM((4, 8, 2, 16, LANES), F32),
                pltpu.VMEM((N2, LANES, 2 * LANES), BF16),
                pltpu.VMEM((2 * NT, LANES), F32),
                pltpu.VMEM((2 * NT, LANES), F32),
            ],
        ),
        name="transform",
    )(rows, local, jnp.asarray(inner_matrix(), BF16), jnp.asarray(tw_cos), jnp.asarray(tw_sin))

    moved = lax.all_to_all(spectrum.reshape(DEVS, 2 * SLOTS, LANES), ALL, 0, 0, tiled=True)

    kl, part = pl.pallas_call(
        filter_kernel,
        out_shape=(
            jax.ShapeDtypeStruct((SLOTS * 2 * CH, KL), BF16),
            jax.ShapeDtypeStruct((DEVS, 128), F32),
        ),
        grid=(4,),
        in_specs=[
            pl.BlockSpec((4, 16, 2, 2 * SLOTS, LANES), lambda i: (0, 0, 0, 0, 0)),
            pl.BlockSpec((8 * KL, NB), lambda i: (i, 0)),
            pl.BlockSpec((64, 128), lambda i: (i, 0)),
            pl.BlockSpec((8, 256), lambda i: (0, 0)),
        ],
        out_specs=(
            pl.BlockSpec((128, KL), lambda i: (i, 0)),
            pl.BlockSpec((DEVS, 128), lambda i: (0, 0)),
        ),
        scratch_shapes=[pltpu.VMEM((128, NB), BF16), pltpu.VMEM((256, 128), F32)],
        name="filter",
    )(moved.reshape(4, 16, 2, 2 * SLOTS, LANES), masked, band_col, band_row)

    shares = lax.all_to_all(part[:, None, :], ALL, 0, 0, tiled=True)
    power = shares.reshape(DEVS, 128).sum(axis=0)[:64].reshape(CH, 8)
    return kl.reshape(SLOTS, 2, CH, KL), power * (NBAND / (NT * KL))


def solution(mesh):
    fine = Mesh(mesh.devices.reshape(4, 16, 2), ALL)
    wide = ("yx", "core")
    placed = (P(None, None, wide, "grp"), P(ALL, None, None), P(), P(), P())
    return jax.shard_map(
        body,
        mesh=fine,
        in_specs=placed,
        out_specs=(P(ALL, None, None, None), P(None, ALL)),
        check_vma=False,
    )
```

```python
import math

import jax
import jax.numpy as jnp
import numpy as np
from jax import lax
from jax.experimental import pallas as pl
from jax.experimental.pallas import tpu as pltpu
from jax.sharding import Mesh
from jax.sharding import PartitionSpec as P

CH = 8
NB = 2048
NT = 4096
KL = 64
KB = 8
NBAND = 1024
NKB = 8

DEVS = 128
SLOTS = NT // DEVS
LANES = 128
N2 = NT // LANES
ALL = ("grp", "yx", "core")
F32 = jnp.float32
BF16 = jnp.bfloat16
NT_DIMS = (((1,), (1,)), ((), ()))


def inner_matrix():
    n = np.arange(LANES)
    angle = 2.0 * np.pi * ((n[:, None] * n[None, :]) % LANES) / LANES
    c, s = np.cos(angle) / math.sqrt(NT), np.sin(angle) / math.sqrt(NT)
    re = np.concatenate([c, s], axis=1)
    im = np.concatenate([-s, c], axis=1)
    return np.stack([re, im], axis=1).reshape(2 * LANES, 2 * LANES)


def twiddles():
    z = np.arange(4)[:, None, None]
    m2 = np.arange(N2)[None, :, None]
    t1 = np.arange(LANES)[None, None, :]
    angle = 2.0 * np.pi * ((m2 * t1 + z * m2 * (NT // 4)) % NT) / NT
    angle = angle.reshape(4 * N2, LANES)
    return np.cos(angle).astype(np.float32), np.sin(angle).astype(np.float32)


def cmul_const(re, im, angle):
    c, s = math.cos(angle), math.sin(angle)
    return re * c + im * s, im * c - re * s


def dft4(x):
    (ar, ai), (br, bi), (cr, ci), (dr, di) = x
    pr, pi, qr, qi = ar + cr, ai + ci, ar - cr, ai - ci
    rr, ri, sr, si = br + dr, bi + di, br - dr, bi - di
    return [(pr + rr, pi + ri), (qr + si, qi - sr), (pr - rr, pi - ri), (qr - si, qi + sr)]


def dft8(x):
    even = dft4([x[0], x[2], x[4], x[6]])
    odd = dft4([x[1], x[3], x[5], x[7]])
    h = math.sqrt(0.5)
    o0 = odd[0]
    o1 = ((odd[1][0] + odd[1][1]) * h, (odd[1][1] - odd[1][0]) * h)
    o2 = (odd[2][1], -odd[2][0])
    o3 = ((odd[3][1] - odd[3][0]) * h, (odd[3][0] + odd[3][1]) * -h)
    lo, hi = [], []
    for (er, ei), (pr, pi) in zip(even, [o0, o1, o2, o3]):
        lo.append((er + pr, ei + pi))
        hi.append((er - pr, ei - pi))
    return lo + hi


HOPS = tuple((core, z) for core in range(2) for z in range(4))


def split_kernel(place_ref, v_ref, *refs):
    outs, sems = refs[:-1], refs[-1]
    copies = []
    for i, (core, z) in enumerate(HOPS[1:]):
        to = (place_ref[0] + z) % 4 * 2 + (place_ref[1] + core) % 2
        for p in range(2):
            copies.append(
                pltpu.make_async_copy(v_ref.at[p, to], outs[i].at[p], sems.at[2 * i + p])
            )
    for copy in copies:
        copy.start()
    for copy in copies:
        copy.wait()


def outer_rows(place_ref, blocks, d_ref, mid, twc_ref, tws_ref, core):
    table = pl.multiple_of(place_ref[0] * N2, N2)
    first = (place_ref[1] + core) % 2 * 64

    def outer(rg, carry):
        r0 = pl.multiple_of(rg * 16, 16)
        for j in range(8):
            cols = slice(j * LANES, (j + 1) * LANES)
            x = [
                tuple(blocks[4 * core + z][p, pl.ds(r0, 16), cols].astype(F32) for p in range(2))
                for z in (0, 3, 2, 1)
            ]
            for q, (re, im) in enumerate(dft4(x)):
                if j * q:
                    re, im = cmul_const(re, im, 2.0 * math.pi * j * q / N2)
                mid[q, j, 0] = re
                mid[q, j, 1] = im
        out0 = pl.multiple_of(first + rg * 16, 16)
        for q in range(4):
            for half in range(2):
                rows = slice(half * 8, half * 8 + 8)
                y = dft8([(mid[q, j, 0, rows], mid[q, j, 1, rows]) for j in range(8)])
                for p, (re, im) in enumerate(y):
                    m2 = q + 4 * p
                    c = twc_ref[pl.ds(table + m2, 1), :]
                    s = tws_ref[pl.ds(table + m2, 1), :]
                    mid[q, p, 0, rows] = re * c + im * s
                    mid[q, p, 1, rows] = im * c - re * s
            for p in range(8):
                for part in range(2):
                    d_ref[q + 4 * p, pl.ds(out0, 16), part * LANES : (part + 1) * LANES] = mid[
                        q, p, part
                    ].astype(BF16)
        return carry

    lax.fori_loop(0, 4, outer, 0)


PIECE = 1024


def invert_kernel(place_ref, from_ref, v_ref, to_ref, own_ref, sems):
    own = place_ref[0] * 2 + place_ref[1]
    copies = [
        pltpu.make_async_copy(v_ref.at[p, own], own_ref.at[p], sems.at[p]) for p in range(2)
    ]
    for copy in copies:
        copy.start()

    def step(i, carry):
        for u in range(16):
            s = i * 16 + u
            to_ref[from_ref[s]] = 2 * s
        return carry

    lax.fori_loop(0, NT // 16, step, 0)
    for copy in copies:
        copy.wait()


def transform_kernel(place_ref, to_ref, w_ref, twc_ref, tws_ref, *refs):
    blocks, (o_ref, mid, d_ref, even, odd, picked, narrow, sems) = refs[:8], refs[8:]
    for core in range(2):
        outer_rows(place_ref, blocks, d_ref, mid, twc_ref, tws_ref, core)

    def inner(m2, spec):
        spec[...] = lax.dot_general(w_ref[...], d_ref[m2], NT_DIMS, preferred_element_type=F32)

    def scatter(m2, spec):
        for u in range(LANES):
            to = pl.multiple_of(to_ref[m2 * LANES + u], 2)
            picked[pl.ds(to, 2), :] = spec[2 * u : 2 * u + 2, :]

    inner(0, even)
    for m2 in range(N2):
        if m2 + 1 < N2:
            inner(m2 + 1, even if m2 % 2 else odd)
        scatter(m2, odd if m2 % 2 else even)

    def piece(i):
        where = pl.ds(pl.multiple_of(i * PIECE, PIECE), PIECE)
        return pltpu.make_async_copy(narrow.at[where, :], o_ref.at[where, :], sems.at[i])

    def send(i, carry):
        where = pl.ds(pl.multiple_of(i * PIECE, PIECE), PIECE)
        narrow[where, :] = picked[where, :].astype(BF16)
        piece(i).start()
        return carry

    lax.fori_loop(0, 2 * NT // PIECE, send, 0)
    for i in range(2 * NT // PIECE):
        piece(i).wait()


def table_kernel(
    place_ref, slot_ref, counts_ref, f_ref, band_ref, o_ref, col_ref, hot_ref, f_in, sems
):
    copies = [
        pltpu.make_async_copy(
            f_ref.at[pl.ds(i * 512, 512), :], f_in.at[pl.ds(i * 512, 512), :], sems.at[i]
        )
        for i in range(4)
    ]
    for copy in copies:
        copy.start()
    first = place_ref[0] * SLOTS

    def bands(s, carry):
        m = slot_ref[first + s]
        tile = band_ref[:, pl.ds(pl.multiple_of((m // 128) * 128, 128), 128)]
        one = jnp.where(lax.broadcasted_iota(jnp.int32, (8, 128), 1) == m % 128, tile, 0)
        where = pl.ds(pl.multiple_of(s * 8, 8), 8)
        col_ref[where, :] = jnp.broadcast_to(one.sum(axis=1, keepdims=True), (8, 128))
        return carry

    lax.fori_loop(0, SLOTS, bands, 0)
    owner = col_ref[...] // 8 == lax.broadcasted_iota(jnp.int32, (256, 128), 1)
    hot_ref[...] = jnp.where(owner, 1.0, 0.0).T.astype(BF16)
    column = lax.broadcasted_iota(jnp.int32, (KL, NB), 1)
    for i in range(4):
        copies[i].wait()

        def slot(s, carry):
            where = pl.ds(pl.multiple_of(s * KL, KL), KL)
            keep = column < counts_ref[slot_ref[first + s]]
            f_in[where, :] = jnp.where(keep, f_in[where, :], jnp.zeros((), BF16))
            return carry

        lax.fori_loop(i * 8, i * 8 + 8, slot, 0)
        for j in range(16):
            o_ref[i, j * 128 : (j + 1) * 128, :] = f_in[
                i * 512 : (i + 1) * 512, j * 128 : (j + 1) * 128
            ].T


def split3(x):
    a = x.astype(BF16)
    r = x - a.astype(F32)
    b = r.astype(BF16)
    return a, b, (r - b.astype(F32)).astype(BF16)


def iota(shape, axis):
    return lax.broadcasted_iota(jnp.int32, shape, axis)


def filter_kernel(x_ref, f_hbm, col_ref, hot_ref, kl_ref, band_ref, rhs, data, f_ref, sems):
    copies = [
        pltpu.make_async_copy(
            f_hbm.at[i], f_ref.at[i], sems.at[i]
        )
        for i in range(4)
    ]
    copies[0].start()
    copies[1].start()
    for at in range(4):
        for k in range(16):
            data[:, k * LANES : (k + 1) * LANES] = x_ref[
                :, k, :, at * 16 : (at + 1) * 16, :
            ].reshape(128, LANES)
        copies[at].wait()
        if at < 2:
            copies[at + 2].start()
        acc = lax.dot_general(
            data[...], f_ref[at], (((1,), (0,)), ((), ())), preferred_element_type=F32
        )
        own = ((iota((128, 512), 0) // 2) % 8) == (iota((128, 512), 1) // KL)
        acc = jnp.where(own, acc, 0.0)
        pairs = acc[:, 0:128] + acc[:, 128:256] + acc[:, 256:384] + acc[:, 384:512]
        mine = (pairs[:, :KL] + pairs[:, KL:]).astype(BF16)
        to, frm = iota((128, 128), 0), iota((128, 128), 1)
        order = jnp.where(frm == (to % 8) * 16 + to // 8, 1.0, 0.0).astype(BF16)
        kl_ref[at * 128 : (at + 1) * 128, :] = jnp.dot(
            order, mine, preferred_element_type=F32
        ).astype(BF16)
        power = (acc * acc).reshape(8, 16, 512).sum(axis=1)
        spread = jnp.broadcast_to(power[:, None, :], (8, 8, 512)).reshape(64, 512)
        blocks = jnp.where(iota((64, 512), 1) // KB == iota((64, 512), 0), 1.0, 0.0).astype(BF16)
        table = sum(
            lax.dot_general(blocks, part, NT_DIMS, preferred_element_type=F32)
            for part in split3(spread)
        )
        band = col_ref[at * 64 : (at + 1) * 64, :]
        low = iota((64, 64), 1) % 8
        table = jnp.where((band[:, :64] % 8) == low, table, 0.0)
        rhs[at * 64 : (at + 1) * 64, :] = jnp.concatenate([table, jnp.zeros((64, 64), F32)], axis=1)
    band_ref[...] = sum(
        jnp.dot(hot_ref[...], part, preferred_element_type=F32) for part in split3(rhs[...])
    )


def call(kernel, name, out, inputs, scratch=(), smem=(), anyspace=(), hbm=(), limit=24, **where):
    vmem = pl.BlockSpec(memory_space=pltpu.VMEM)
    specs = [vmem] * len(inputs)
    for i in smem:
        specs[i] = pl.BlockSpec(memory_space=pltpu.SMEM)
    for i in anyspace:
        specs[i] = pl.BlockSpec(memory_space=pltpu.HBM)
    inputs = tuple(
        pltpu.with_memory_space_constraint(x, pltpu.HBM) if i in anyspace and i in hbm else x
        for i, x in enumerate(inputs)
    )
    result = vmem
    if where.get("out_any"):
        result = pl.BlockSpec(memory_space=pltpu.HBM)
    outs = (result,) * len(out) if isinstance(out, tuple) else result
    if where.get("out_smem"):
        outs = (pl.BlockSpec(memory_space=pltpu.SMEM),) + outs[1:]
    return pl.pallas_call(
        kernel,
        out_shape=out,
        in_specs=specs,
        out_specs=outs,
        scratch_shapes=list(scratch),
        compiler_params=pltpu.CompilerParams(vmem_limit_bytes=limit << 20),
        name=name,
    )(*inputs)


def body(visibilities, filters, counts, m_of_slot, band_of_block):
    struct = jax.ShapeDtypeStruct
    dma = pltpu.SemaphoreType.DMA
    group = ("grp", "core")
    spot = jnp.stack([lax.axis_index("grp"), lax.axis_index("core")])
    sent = call(
        split_kernel,
        "split",
        (struct((2, 64, 1024), BF16),) * 7,
        (spot, visibilities),
        [dma((14,))],
        smem=(0,),
        hbm=(1,),
        anyspace=(1,),
        out_any=True,
    )
    local = []
    for i, (core, z) in enumerate(HOPS[1:]):
        hop = [(k, (k // 2 + z) % 4 * 2 + (k + core) % 2) for k in range(8)]
        local.append(lax.ppermute(sent[i], group, hop))

    rows = (m_of_slot % N2) * LANES + m_of_slot // N2
    to, own = call(
        invert_kernel,
        "invert",
        (struct((NT,), jnp.int32), struct((2, 64, 1024), BF16)),
        (spot, rows, visibilities),
        [dma((2,))],
        smem=(0, 1),
        hbm=(2,),
        anyspace=(2,),
        out_smem=True,
        limit=4,
    )
    tables = tuple(jnp.asarray(t) for t in twiddles())
    spectrum = call(
        transform_kernel,
        "transform",
        struct((2 * NT, LANES), BF16),
        (spot, to, jnp.asarray(inner_matrix(), BF16)) + tables + (own,) + tuple(local),
        [
            pltpu.VMEM((4, 8, 2, 16, LANES), F32),
            pltpu.VMEM((N2, LANES, 2 * LANES), BF16),
            pltpu.VMEM((2 * LANES, LANES), F32),
            pltpu.VMEM((2 * LANES, LANES), F32),
            pltpu.VMEM((2 * NT, LANES), F32),
            pltpu.VMEM((2 * NT, LANES), BF16),
            dma((2 * NT // PIECE,)),
        ],
        smem=(0, 1),
        out_any=True,
    )
    moved = lax.all_to_all(spectrum.reshape(DEVS, 2 * SLOTS, LANES), ALL, 0, 0, tiled=True)

    place = lax.axis_index(ALL).reshape(1)
    masked, col, hot = call(
        table_kernel,
        "tables",
        (struct((4, NB, 512), BF16), struct((256, 128), jnp.int32), struct((128, 256), BF16)),
        (place, m_of_slot, counts, filters.reshape(SLOTS * KL, NB), band_of_block.T),
        [pltpu.VMEM((SLOTS * KL, NB), BF16), dma((4,))],
        smem=(0, 1, 2),
        anyspace=(3,),
        hbm=(3,),
    )
    kl, part = call(
        filter_kernel,
        "filter",
        (struct((512, KL), BF16), struct((DEVS, 128), F32)),
        (moved.reshape(4, 16, 2, 2 * SLOTS, LANES), masked, col, hot),
        [
            pltpu.VMEM((256, 128), F32),
            pltpu.VMEM((128, NB), BF16),
            pltpu.VMEM((4, NB, 512), BF16),
            dma((4,)),
        ],
        anyspace=(1,),
        hbm=(1,),
    )
    shares = lax.all_to_all(part[:, None, :], ALL, 0, 0, tiled=True)
    power = shares.reshape(DEVS, 128).sum(axis=0)[:64].reshape(CH, 8)
    return kl.reshape(SLOTS, 2, CH, KL), power * (NBAND / (NT * KL))


def solution(mesh):
    fine = Mesh(mesh.devices.reshape(4, 16, 2), ALL)
    wide = ("yx", "core")
    placed = (P(None, None, wide, "grp"), P(ALL, None, None), P(), P(), P())
    return jax.shard_map(
        body,
        mesh=fine,
        in_specs=placed,
        out_specs=(P(ALL, None, None, None), P(None, ALL)),
        check_vma=False,
    )
```

```python
import functools
import math

import jax
import jax.numpy as jnp
import numpy as np
from jax import lax
from jax.experimental import pallas as pl
from jax.experimental.pallas import tpu as pltpu
from jax.sharding import Mesh
from jax.sharding import PartitionSpec as P

CH = 8
NB = 2048
NT = 4096
KL = 64
KB = 8
NBAND = 1024
NKB = 8

DEVS = 128
SLOTS = NT // DEVS
LANES = 128
N2 = NT // LANES
ALL = ("grp", "yx", "core")
F32 = jnp.float32
BF16 = jnp.bfloat16
NT_DIMS = (((1,), (1,)), ((), ()))


def inner_matrix():
    n = np.arange(LANES)
    angle = 2.0 * np.pi * ((n[:, None] * n[None, :]) % LANES) / LANES
    c, s = np.cos(angle) / math.sqrt(NT), np.sin(angle) / math.sqrt(NT)
    re = np.concatenate([c, s], axis=1)
    im = np.concatenate([-s, c], axis=1)
    return np.stack([re, im], axis=1).reshape(2 * LANES, 2 * LANES)


def twiddles():
    z = np.arange(4)[:, None, None]
    m2 = np.arange(N2)[None, :, None]
    t1 = np.arange(LANES)[None, None, :]
    angle = 2.0 * np.pi * ((m2 * t1 + z * m2 * (NT // 4)) % NT) / NT
    angle = angle.reshape(4 * N2, LANES)
    return np.cos(angle).astype(np.float32), np.sin(angle).astype(np.float32)


def cmul_const(re, im, angle):
    c, s = math.cos(angle), math.sin(angle)
    return re * c + im * s, im * c - re * s


def dft4(x):
    (ar, ai), (br, bi), (cr, ci), (dr, di) = x
    pr, pi, qr, qi = ar + cr, ai + ci, ar - cr, ai - ci
    rr, ri, sr, si = br + dr, bi + di, br - dr, bi - di
    return [(pr + rr, pi + ri), (qr + si, qi - sr), (pr - rr, pi - ri), (qr - si, qi + sr)]


def dft8(x):
    even = dft4([x[0], x[2], x[4], x[6]])
    odd = dft4([x[1], x[3], x[5], x[7]])
    h = math.sqrt(0.5)
    o0 = odd[0]
    o1 = ((odd[1][0] + odd[1][1]) * h, (odd[1][1] - odd[1][0]) * h)
    o2 = (odd[2][1], -odd[2][0])
    o3 = ((odd[3][1] - odd[3][0]) * h, (odd[3][0] + odd[3][1]) * -h)
    lo, hi = [], []
    for (er, ei), (pr, pi) in zip(even, [o0, o1, o2, o3]):
        lo.append((er + pr, ei + pi))
        hi.append((er - pr, ei - pi))
    return lo + hi


ORDER = ((0, 1), (0, 3), (0, 2), (1, 2), (1, 1), (1, 3), (1, 0))
HOPS = tuple((core, z) for core in range(2) for z in range(4))


def split_kernel(hops, place_ref, v_ref, *refs):
    outs, sems = refs[:-1], refs[-1]
    copies = []
    for i, (core, z) in enumerate(hops):
        to = (place_ref[0] + z) % 4 * 2 + (place_ref[1] + core) % 2
        for p in range(2):
            copies.append(
                pltpu.make_async_copy(v_ref.at[p, to], outs[i].at[p], sems.at[2 * i + p])
            )
    for copy in copies:
        copy.start()
    for copy in copies:
        copy.wait()


def outer_rows(blocks, d_ref, mid, twc_ref, tws_ref, place_ref):
    table = pl.multiple_of(place_ref[0] * N2, N2)

    def outer(rg, carry):
        r0 = pl.multiple_of(rg * 16, 16)
        for j in range(8):
            cols = slice(j * LANES, (j + 1) * LANES)
            x = [
                tuple(blocks[z][p, pl.ds(r0, 16), cols].astype(F32) for p in range(2))
                for z in (0, 3, 2, 1)
            ]
            for q, (re, im) in enumerate(dft4(x)):
                if j * q:
                    re, im = cmul_const(re, im, 2.0 * math.pi * j * q / N2)
                mid[q, j, 0] = re
                mid[q, j, 1] = im
        out0 = pl.multiple_of(rg * 16, 16)
        for q in range(4):
            for half in range(2):
                rows = slice(half * 8, half * 8 + 8)
                y = dft8([(mid[q, j, 0, rows], mid[q, j, 1, rows]) for j in range(8)])
                for p, (re, im) in enumerate(y):
                    m2 = q + 4 * p
                    c = twc_ref[pl.ds(table + m2, 1), :]
                    s = tws_ref[pl.ds(table + m2, 1), :]
                    mid[q, p, 0, rows] = re * c + im * s
                    mid[q, p, 1, rows] = im * c - re * s
            for p in range(8):
                for part in range(2):
                    d_ref[q + 4 * p, pl.ds(out0, 16), part * LANES : (part + 1) * LANES] = mid[
                        q, p, part
                    ].astype(BF16)
        return carry

    lax.fori_loop(0, 4, outer, 0)


PIECE = 1024


def invert_kernel(place_ref, from_ref, v_ref, to_ref, own_ref, sems):
    own = place_ref[0] * 2 + place_ref[1]
    copies = [
        pltpu.make_async_copy(v_ref.at[p, own], own_ref.at[p], sems.at[p]) for p in range(2)
    ]
    for copy in copies:
        copy.start()

    def step(i, carry):
        for u in range(16):
            s = i * 16 + u
            to_ref[from_ref[s]] = 2 * s
        return carry

    lax.fori_loop(0, NT // 16, step, 0)
    for copy in copies:
        copy.wait()


def early_kernel(place_ref, twc_ref, tws_ref, *refs):
    blocks, (d_ref, mid) = refs[:4], refs[4:]
    outer_rows(blocks, d_ref, mid, twc_ref, tws_ref, place_ref)


def transform_kernel(place_ref, to_ref, w_ref, twc_ref, tws_ref, same_ref, *refs):
    blocks, (o_ref, mid, d_ref, even, odd, picked, narrow, sems, rows, fetched) = refs[:4], refs[4:]
    fetch = pltpu.make_async_copy(to_ref, rows.at[pl.ds(0, NT)], fetched.at[0])
    fetch.start()
    outer_rows(blocks, d_ref, mid, twc_ref, tws_ref, place_ref)
    shift = place_ref[1]

    def inner(m2, spec):
        both = jnp.where(shift == 0, same_ref[m2], d_ref[m2]), jnp.where(
            shift == 0, d_ref[m2], same_ref[m2]
        )
        data = jnp.concatenate(both, axis=0)
        spec[...] = lax.dot_general(w_ref[...], data, NT_DIMS, preferred_element_type=F32)

    def scatter(m2, spec):
        for u in range(LANES):
            if u % 32 == 0:
                rows[NT + place_ref[0]] = u
            to = pl.multiple_of(rows[m2 * LANES + u], 2)
            picked[pl.ds(to, 2), :] = spec[2 * u : 2 * u + 2, :]

    fetch.wait()
    inner(0, even)
    for m2 in range(N2):
        if m2 + 1 < N2:
            inner(m2 + 1, even if m2 % 2 else odd)
        scatter(m2, odd if m2 % 2 else even)

    def piece(i):
        where = pl.ds(pl.multiple_of(i * PIECE, PIECE), PIECE)
        return pltpu.make_async_copy(narrow.at[where, :], o_ref.at[where, :], sems.at[i])

    def send(i, carry):
        where = pl.ds(pl.multiple_of(i * PIECE, PIECE), PIECE)
        narrow[where, :] = picked[where, :].astype(BF16)
        piece(i).start()
        return carry

    lax.fori_loop(0, 2 * NT // PIECE, send, 0)
    for i in range(2 * NT // PIECE):
        piece(i).wait()


def table_kernel(
    place_ref, slot_ref, counts_ref, f_ref, band_ref, o_ref, col_ref, hot_ref, f_in, sems
):
    copies = [
        pltpu.make_async_copy(
            f_ref.at[pl.ds(i * 512, 512), :], f_in.at[pl.ds(i * 512, 512), :], sems.at[i]
        )
        for i in range(4)
    ]
    for copy in copies:
        copy.start()
    first = place_ref[0] * SLOTS

    def bands(s, carry):
        m = slot_ref[first + s]
        tile = band_ref[:, pl.ds(pl.multiple_of((m // 128) * 128, 128), 128)]
        one = jnp.where(lax.broadcasted_iota(jnp.int32, (8, 128), 1) == m % 128, tile, 0)
        where = pl.ds(pl.multiple_of(s * 8, 8), 8)
        col_ref[where, :] = jnp.broadcast_to(one.sum(axis=1, keepdims=True), (8, 128))
        return carry

    lax.fori_loop(0, SLOTS, bands, 0)
    owner = col_ref[...] // 8 == lax.broadcasted_iota(jnp.int32, (256, 128), 1)
    hot_ref[...] = jnp.where(owner, 1.0, 0.0).T.astype(BF16)
    column = lax.broadcasted_iota(jnp.int32, (KL, NB), 1)
    for i in range(4):
        copies[i].wait()

        def slot(s, carry):
            where = pl.ds(pl.multiple_of(s * KL, KL), KL)
            keep = column < counts_ref[slot_ref[first + s]]
            f_in[where, :] = jnp.where(keep, f_in[where, :], jnp.zeros((), BF16))
            return carry

        lax.fori_loop(i * 8, i * 8 + 8, slot, 0)
        for j in range(16):
            o_ref[i, j * 128 : (j + 1) * 128, :] = f_in[
                i * 512 : (i + 1) * 512, j * 128 : (j + 1) * 128
            ].T


def split3(x):
    a = x.astype(BF16)
    r = x - a.astype(F32)
    b = r.astype(BF16)
    return a, b, (r - b.astype(F32)).astype(BF16)


def iota(shape, axis):
    return lax.broadcasted_iota(jnp.int32, shape, axis)


def filter_kernel(x_ref, f_hbm, col_ref, hot_ref, kl_ref, band_ref, rhs, data, f_ref, sems):
    copies = [
        pltpu.make_async_copy(
            f_hbm.at[i], f_ref.at[i], sems.at[i]
        )
        for i in range(4)
    ]
    copies[0].start()
    copies[1].start()
    copies[2].start()
    for at in range(4):
        for k in range(16):
            data[:, k * LANES : (k + 1) * LANES] = x_ref[
                :, k, :, at * 16 : (at + 1) * 16, :
            ].reshape(128, LANES)
        copies[at].wait()
        if at == 0:
            copies[3].start()
        acc = lax.dot_general(
            data[...], f_ref[at], (((1,), (0,)), ((), ())), preferred_element_type=F32
        )
        own = ((iota((128, 512), 0) // 2) % 8) == (iota((128, 512), 1) // KL)
        acc = jnp.where(own, acc, 0.0)
        pairs = acc[:, 0:128] + acc[:, 128:256] + acc[:, 256:384] + acc[:, 384:512]
        mine = (pairs[:, :KL] + pairs[:, KL:]).astype(BF16)
        to, frm = iota((128, 128), 0), iota((128, 128), 1)
        order = jnp.where(frm == (to % 8) * 16 + to // 8, 1.0, 0.0).astype(BF16)
        kl_ref[at * 128 : (at + 1) * 128, :] = jnp.dot(
            order, mine, preferred_element_type=F32
        ).astype(BF16)
        power = (acc * acc).reshape(8, 16, 512).sum(axis=1)
        spread = jnp.broadcast_to(power[:, None, :], (8, 8, 512)).reshape(64, 512)
        blocks = jnp.where(iota((64, 512), 1) // KB == iota((64, 512), 0), 1.0, 0.0).astype(BF16)
        table = sum(
            lax.dot_general(blocks, part, NT_DIMS, preferred_element_type=F32)
            for part in split3(spread)
        )
        band = col_ref[at * 64 : (at + 1) * 64, :]
        low = iota((64, 64), 1) % 8
        table = jnp.where((band[:, :64] % 8) == low, table, 0.0)
        rhs[at * 64 : (at + 1) * 64, :] = jnp.concatenate([table, jnp.zeros((64, 64), F32)], axis=1)
    band_ref[...] = sum(
        jnp.dot(hot_ref[...], part, preferred_element_type=F32) for part in split3(rhs[...])
    )


def total_kernel(x_ref, o_ref):
    total = jnp.broadcast_to(x_ref[...].sum(axis=0, keepdims=True), (8, 128))
    total = jnp.where(iota((8, 128), 1) // 8 == iota((8, 128), 0), total, 0.0)
    pick = jnp.where(iota((128, 128), 0) % 8 == iota((128, 128), 1), 1.0, 0.0).astype(BF16)
    power = sum(jnp.dot(part, pick, preferred_element_type=F32) for part in split3(total))
    o_ref[...] = power[:, :8] * (NBAND / (NT * KL))


def call(kernel, name, out, inputs, scratch=(), smem=(), anyspace=(), hbm=(), limit=24, **where):
    vmem = pl.BlockSpec(memory_space=pltpu.VMEM)
    specs = [vmem] * len(inputs)
    for i in smem:
        specs[i] = pl.BlockSpec(memory_space=pltpu.SMEM)
    for i in anyspace:
        specs[i] = pl.BlockSpec(memory_space=pltpu.HBM)
    inputs = tuple(
        pltpu.with_memory_space_constraint(x, pltpu.HBM) if i in anyspace and i in hbm else x
        for i, x in enumerate(inputs)
    )
    result = vmem
    if where.get("out_any"):
        result = pl.BlockSpec(memory_space=pltpu.HBM)
    outs = (result,) * len(out) if isinstance(out, tuple) else result
    if where.get("out_smem"):
        outs = (pl.BlockSpec(memory_space=pltpu.SMEM),) + outs[1:]
    return pl.pallas_call(
        kernel,
        out_shape=out,
        in_specs=specs,
        out_specs=outs,
        scratch_shapes=list(scratch),
        compiler_params=pltpu.CompilerParams(vmem_limit_bytes=limit << 20),
        name=name,
    )(*inputs)


def body(visibilities, filters, counts, m_of_slot, band_of_block):
    struct = jax.ShapeDtypeStruct
    dma = pltpu.SemaphoreType.DMA
    group = ("grp", "core")
    spot = jnp.stack([lax.axis_index("grp"), lax.axis_index("core")])
    blocks = []
    for core, z in ORDER[:2]:
        to = (spot[0] + z) % 4 * 2 + (spot[1] + core) % 2
        blocks.append(lax.dynamic_index_in_dim(visibilities, to, 1, keepdims=False))
    sent = call(
        functools.partial(split_kernel, ORDER[2:]),
        "split",
        (struct((2, 64, 1024), BF16),) * 5,
        (spot, visibilities),
        [dma((10,))],
        smem=(0,),
        hbm=(1,),
        anyspace=(1,),
        out_any=True,
    )
    blocks += sent
    got = {}
    for (core, z), block in zip(ORDER, blocks):
        hop = [(k, (k // 2 + z) % 4 * 2 + (k + core) % 2) for k in range(8)]
        got[core, z] = lax.ppermute(block, group, hop)
    local = [got[hop] for hop in HOPS[1:]]

    rows = (m_of_slot % N2) * LANES + m_of_slot // N2
    to, own = call(
        invert_kernel,
        "invert",
        (struct((NT,), jnp.int32), struct((2, 64, 1024), BF16)),
        (spot, rows, visibilities),
        [dma((2,))],
        smem=(0, 1),
        hbm=(2,),
        anyspace=(2,),
        out_smem=True,
        limit=4,
    )
    tables = tuple(jnp.asarray(t) for t in twiddles())
    mid = pltpu.VMEM((4, 8, 2, 16, LANES), F32)
    same = call(
        early_kernel,
        "early",
        struct((N2, 64, 2 * LANES), BF16),
        (spot,) + tables + (own,) + tuple(local[:3]),
        [mid],
        smem=(0,),
    )
    spectrum = call(
        transform_kernel,
        "transform",
        struct((2 * NT, LANES), BF16),
        (spot, to, jnp.asarray(inner_matrix(), BF16)) + tables + (same,) + tuple(local[3:]),
        [
            mid,
            pltpu.VMEM((N2, 64, 2 * LANES), BF16),
            pltpu.VMEM((2 * LANES, LANES), F32),
            pltpu.VMEM((2 * LANES, LANES), F32),
            pltpu.VMEM((2 * NT, LANES), F32),
            pltpu.VMEM((2 * NT, LANES), BF16),
            dma((2 * NT // PIECE,)),
            pltpu.SMEM((NT + 1024,), jnp.int32),
            dma((1,)),
        ],
        smem=(0,),
        anyspace=(1,),
        out_any=True,
    )
    moved = lax.all_to_all(spectrum.reshape(DEVS, 2 * SLOTS, LANES), ALL, 0, 0, tiled=True)

    place = lax.axis_index(ALL).reshape(1)
    masked, col, hot = call(
        table_kernel,
        "tables",
        (struct((4, NB, 512), BF16), struct((256, 128), jnp.int32), struct((128, 256), BF16)),
        (place, m_of_slot, counts, filters.reshape(SLOTS * KL, NB), band_of_block.T),
        [pltpu.VMEM((SLOTS * KL, NB), BF16), dma((4,))],
        smem=(0, 1, 2),
        anyspace=(3,),
        hbm=(3,),
    )
    kl, part = call(
        filter_kernel,
        "filter",
        (struct((512, KL), BF16), struct((DEVS, 128), F32)),
        (moved.reshape(4, 16, 2, 2 * SLOTS, LANES), masked, col, hot),
        [
            pltpu.VMEM((256, 128), F32),
            pltpu.VMEM((128, NB), BF16),
            pltpu.VMEM((4, NB, 512), BF16),
            dma((4,)),
        ],
        anyspace=(1,),
        hbm=(1,),
    )
    shares = lax.all_to_all(part[:, None, :], ALL, 0, 0, tiled=True)
    power = call(total_kernel, "total", struct((CH, 8), F32), (shares.reshape(DEVS, 128),), limit=4)
    return kl.reshape(SLOTS, 2, CH, KL), power


def solution(mesh):
    fine = Mesh(mesh.devices.reshape(4, 16, 2), ALL)
    wide = ("yx", "core")
    placed = (P(None, None, wide, "grp"), P(ALL, None, None), P(), P(), P())
    return jax.shard_map(
        body,
        mesh=fine,
        in_specs=placed,
        out_specs=(P(ALL, None, None, None), P(None, ALL)),
        check_vma=False,
    )
```

```python
import functools
import math

import jax
import jax.numpy as jnp
import numpy as np
from jax import lax
from jax.experimental import pallas as pl
from jax.experimental.pallas import tpu as pltpu
from jax.sharding import Mesh
from jax.sharding import PartitionSpec as P

CH = 8
NB = 2048
NT = 4096
KL = 64
KB = 8
NBAND = 1024
NKB = 8

DEVS = 128
SLOTS = NT // DEVS
LANES = 128
N2 = NT // LANES
ALL = ("grp", "yx", "core")
F32 = jnp.float32
BF16 = jnp.bfloat16
NT_DIMS = (((1,), (1,)), ((), ()))


def inner_matrix():
    n = np.arange(LANES)
    angle = 2.0 * np.pi * ((n[:, None] * n[None, :]) % LANES) / LANES
    c, s = np.cos(angle) / math.sqrt(NT), np.sin(angle) / math.sqrt(NT)
    re = np.concatenate([c, s], axis=1)
    im = np.concatenate([-s, c], axis=1)
    return np.stack([re, im], axis=1).reshape(2 * LANES, 2 * LANES)


def twiddles():
    z = np.arange(4)[:, None, None]
    m2 = np.arange(N2)[None, :, None]
    t1 = np.arange(LANES)[None, None, :]
    angle = 2.0 * np.pi * ((m2 * t1 + z * m2 * (NT // 4)) % NT) / NT
    angle = angle.reshape(4 * N2, LANES)
    return np.cos(angle).astype(np.float32), np.sin(angle).astype(np.float32)


def cmul_const(re, im, angle):
    c, s = math.cos(angle), math.sin(angle)
    return re * c + im * s, im * c - re * s


def dft4(x):
    (ar, ai), (br, bi), (cr, ci), (dr, di) = x
    pr, pi, qr, qi = ar + cr, ai + ci, ar - cr, ai - ci
    rr, ri, sr, si = br + dr, bi + di, br - dr, bi - di
    return [(pr + rr, pi + ri), (qr + si, qi - sr), (pr - rr, pi - ri), (qr - si, qi + sr)]


def dft8(x):
    even = dft4([x[0], x[2], x[4], x[6]])
    odd = dft4([x[1], x[3], x[5], x[7]])
    h = math.sqrt(0.5)
    o0 = odd[0]
    o1 = ((odd[1][0] + odd[1][1]) * h, (odd[1][1] - odd[1][0]) * h)
    o2 = (odd[2][1], -odd[2][0])
    o3 = ((odd[3][1] - odd[3][0]) * h, (odd[3][0] + odd[3][1]) * -h)
    lo, hi = [], []
    for (er, ei), (pr, pi) in zip(even, [o0, o1, o2, o3]):
        lo.append((er + pr, ei + pi))
        hi.append((er - pr, ei - pi))
    return lo + hi


ORDER = ((0, 1), (0, 3), (0, 2), (1, 2), (1, 1), (1, 3), (1, 0))
HEAD = 1024
HOPS = tuple((core, z) for core in range(2) for z in range(4))


def split_kernel(hops, place_ref, v_ref, *refs):
    outs, sems = refs[:-1], refs[-1]
    copies = []
    for i, (core, z) in enumerate(hops):
        to = (place_ref[0] + z) % 4 * 2 + (place_ref[1] + core) % 2
        for p in range(2):
            copies.append(
                pltpu.make_async_copy(v_ref.at[p, to], outs[i].at[p], sems.at[2 * i + p])
            )
    for copy in copies:
        copy.start()
    for copy in copies:
        copy.wait()


def outer_rows(blocks, d_ref, mid, twc_ref, tws_ref, place_ref):
    table = pl.multiple_of(place_ref[0] * N2, N2)

    def outer(rg, carry):
        r0 = pl.multiple_of(rg * 16, 16)
        for j in range(8):
            cols = slice(j * LANES, (j + 1) * LANES)
            x = [
                tuple(blocks[z][p, pl.ds(r0, 16), cols].astype(F32) for p in range(2))
                for z in (0, 3, 2, 1)
            ]
            for q, (re, im) in enumerate(dft4(x)):
                if j * q:
                    re, im = cmul_const(re, im, 2.0 * math.pi * j * q / N2)
                mid[q, j, 0] = re
                mid[q, j, 1] = im
        out0 = pl.multiple_of(rg * 16, 16)
        for q in range(4):
            for half in range(2):
                rows = slice(half * 8, half * 8 + 8)
                y = dft8([(mid[q, j, 0, rows], mid[q, j, 1, rows]) for j in range(8)])
                for p, (re, im) in enumerate(y):
                    m2 = q + 4 * p
                    c = twc_ref[pl.ds(table + m2, 1), :]
                    s = tws_ref[pl.ds(table + m2, 1), :]
                    mid[q, p, 0, rows] = re * c + im * s
                    mid[q, p, 1, rows] = im * c - re * s
            for p in range(8):
                for part in range(2):
                    d_ref[q + 4 * p, pl.ds(out0, 16), part * LANES : (part + 1) * LANES] = mid[
                        q, p, part
                    ].astype(BF16)
        return carry

    lax.fori_loop(0, 4, outer, 0)


PIECE = 512


def invert_kernel(place_ref, from_ref, v_ref, to_ref, own_ref, sems):
    own = place_ref[0] * 2 + place_ref[1]
    copies = [
        pltpu.make_async_copy(v_ref.at[p, own], own_ref.at[p], sems.at[p]) for p in range(2)
    ]
    for copy in copies:
        copy.start()

    def step(i, carry):
        for u in range(16):
            s = i * 16 + u
            to_ref[from_ref[s]] = 2 * s
        return carry

    lax.fori_loop(0, NT // 16, step, 0)
    for copy in copies:
        copy.wait()


def early_kernel(place_ref, twc_ref, tws_ref, *refs):
    blocks, (d_ref, mid) = refs[:4], refs[4:]
    outer_rows(blocks, d_ref, mid, twc_ref, tws_ref, place_ref)


def transform_kernel(place_ref, to_ref, w_ref, twc_ref, tws_ref, same_ref, *refs):
    blocks, (o_ref, mid, d_ref, even, odd, picked, narrow, sems, rows, fetched) = refs[:4], refs[4:]
    fetch = pltpu.make_async_copy(to_ref, rows.at[pl.ds(0, NT)], fetched.at[0])
    fetch.start()
    outer_rows(blocks, d_ref, mid, twc_ref, tws_ref, place_ref)
    shift = place_ref[1]

    def inner(m2, spec):
        both = jnp.where(shift == 0, same_ref[m2], d_ref[m2]), jnp.where(
            shift == 0, d_ref[m2], same_ref[m2]
        )
        data = jnp.concatenate(both, axis=0)
        spec[...] = lax.dot_general(w_ref[...], data, NT_DIMS, preferred_element_type=F32)

    def scatter(m2, spec):
        for u in range(LANES):
            if u % 32 == 0:
                rows[NT + place_ref[0]] = u
            to = pl.multiple_of(rows[m2 * LANES + u], 2)
            picked[pl.ds(to, 2), :] = spec[2 * u : 2 * u + 2, :]

    fetch.wait()
    inner(0, even)
    for m2 in range(N2):
        if m2 + 1 < N2:
            inner(m2 + 1, even if m2 % 2 else odd)
        scatter(m2, odd if m2 % 2 else even)

    def piece(i):
        where = pl.ds(pl.multiple_of(i * PIECE, PIECE), PIECE)
        return pltpu.make_async_copy(narrow.at[where, :], o_ref.at[where, :], sems.at[i])

    def send(i, carry):
        where = pl.ds(pl.multiple_of(i * PIECE, PIECE), PIECE)
        narrow[where, :] = picked[where, :].astype(BF16)
        piece(i).start()
        return carry

    lax.fori_loop(0, 2 * NT // PIECE, send, 0)
    for i in range(2 * NT // PIECE):
        piece(i).wait()


def table_kernel(
    place_ref, slot_ref, counts_ref, f_ref, band_ref, head_ref, o_ref, col_ref, hot_ref, f_in, sems
):
    copies = [
        pltpu.make_async_copy(
            f_ref.at[pl.ds(i * 512, 512), :], f_in.at[pl.ds(i * 512, 512), :], sems.at[i]
        )
        for i in range(4)
    ]
    for copy in copies:
        copy.start()
    first = place_ref[0] * SLOTS

    def bands(s, carry):
        m = slot_ref[first + s]
        tile = band_ref[:, pl.ds(pl.multiple_of((m // 128) * 128, 128), 128)]
        one = jnp.where(lax.broadcasted_iota(jnp.int32, (8, 128), 1) == m % 128, tile, 0)
        where = pl.ds(pl.multiple_of(s * 8, 8), 8)
        col_ref[where, :] = jnp.broadcast_to(one.sum(axis=1, keepdims=True), (8, 128))
        return carry

    lax.fori_loop(0, SLOTS, bands, 0)
    owner = col_ref[...] // 8 == lax.broadcasted_iota(jnp.int32, (256, 128), 1)
    hot_ref[...] = jnp.where(owner, 1.0, 0.0).T.astype(BF16)
    column = lax.broadcasted_iota(jnp.int32, (KL, NB), 1)
    for i in range(4):
        copies[i].wait()

        def slot(s, carry):
            where = pl.ds(pl.multiple_of(s * KL, KL), KL)
            keep = column < counts_ref[slot_ref[first + s]]
            f_in[where, :] = jnp.where(keep, f_in[where, :], jnp.zeros((), BF16))
            return carry

        lax.fori_loop(i * 8, i * 8 + 8, slot, 0)
        for j in range(16):
            block = f_in[i * 512 : (i + 1) * 512, j * 128 : (j + 1) * 128].T
            row = i * NB + j * 128
            if row < HEAD:
                head_ref[row : row + 128, :] = block
            else:
                o_ref[row - HEAD : row - HEAD + 128, :] = block


def split3(x):
    a = x.astype(BF16)
    r = x - a.astype(F32)
    b = r.astype(BF16)
    return a, b, (r - b.astype(F32)).astype(BF16)


def iota(shape, axis):
    return lax.broadcasted_iota(jnp.int32, shape, axis)


def filter_kernel(x_ref, head_ref, f_hbm, col_ref, hot_ref, kl_ref, band_ref, rhs, data, f_ref, sems):
    starts = (0, NB - HEAD, 2 * NB - HEAD, 3 * NB - HEAD, 4 * NB - HEAD)
    copies = [
        pltpu.make_async_copy(
            f_hbm.at[pl.ds(starts[i], starts[i + 1] - starts[i])],
            f_ref.at[pl.ds(starts[i], starts[i + 1] - starts[i])],
            sems.at[i],
        )
        for i in range(4)
    ]
    copies[0].start()
    copies[1].start()
    copies[2].start()
    copies[3].start()
    for at in range(4):
        for k in range(16):
            data[:, k * LANES : (k + 1) * LANES] = x_ref[
                :, k, :, at * 16 : (at + 1) * 16, :
            ].reshape(128, LANES)
        skip = HEAD if at == 0 else 0
        part = 0.0
        if skip:
            part = jnp.dot(data[:, :skip], head_ref[...], preferred_element_type=F32)
        copies[at].wait()
        acc = part + jnp.dot(
            data[:, skip:], f_ref[starts[at] : starts[at + 1], :], preferred_element_type=F32
        )
        own = ((iota((128, 512), 0) // 2) % 8) == (iota((128, 512), 1) // KL)
        acc = jnp.where(own, acc, 0.0)
        pairs = acc[:, 0:128] + acc[:, 128:256] + acc[:, 256:384] + acc[:, 384:512]
        mine = (pairs[:, :KL] + pairs[:, KL:]).astype(BF16)
        to, frm = iota((128, 128), 0), iota((128, 128), 1)
        order = jnp.where(frm == (to % 8) * 16 + to // 8, 1.0, 0.0).astype(BF16)
        kl_ref[at * 128 : (at + 1) * 128, :] = jnp.dot(
            order, mine, preferred_element_type=F32
        ).astype(BF16)
        power = (acc * acc).reshape(8, 16, 512).sum(axis=1)
        spread = jnp.broadcast_to(power[:, None, :], (8, 8, 512)).reshape(64, 512)
        blocks = jnp.where(iota((64, 512), 1) // KB == iota((64, 512), 0), 1.0, 0.0).astype(BF16)
        table = sum(
            lax.dot_general(blocks, part, NT_DIMS, preferred_element_type=F32)
            for part in split3(spread)
        )
        band = col_ref[at * 64 : (at + 1) * 64, :]
        low = iota((64, 64), 1) % 8
        table = jnp.where((band[:, :64] % 8) == low, table, 0.0)
        rhs[at * 64 : (at + 1) * 64, :] = jnp.concatenate([table, jnp.zeros((64, 64), F32)], axis=1)
    band_ref[...] = sum(
        jnp.dot(hot_ref[...], part, preferred_element_type=F32) for part in split3(rhs[...])
    )


def total_kernel(x_ref, o_ref):
    total = jnp.broadcast_to(x_ref[...].sum(axis=0, keepdims=True), (8, 128))
    total = jnp.where(iota((8, 128), 1) // 8 == iota((8, 128), 0), total, 0.0)
    pick = jnp.where(iota((128, 128), 0) % 8 == iota((128, 128), 1), 1.0, 0.0).astype(BF16)
    power = sum(jnp.dot(part, pick, preferred_element_type=F32) for part in split3(total))
    o_ref[...] = power[:, :8] * (NBAND / (NT * KL))


def call(kernel, name, out, inputs, scratch=(), smem=(), anyspace=(), hbm=(), limit=24, **where):
    vmem = pl.BlockSpec(memory_space=pltpu.VMEM)
    specs = [vmem] * len(inputs)
    for i in smem:
        specs[i] = pl.BlockSpec(memory_space=pltpu.SMEM)
    for i in anyspace:
        specs[i] = pl.BlockSpec(memory_space=pltpu.HBM)
    inputs = tuple(
        pltpu.with_memory_space_constraint(x, pltpu.HBM) if i in anyspace and i in hbm else x
        for i, x in enumerate(inputs)
    )
    result = vmem
    if where.get("out_any"):
        result = pl.BlockSpec(memory_space=pltpu.HBM)
    outs = (result,) * len(out) if isinstance(out, tuple) else result
    if where.get("out_smem"):
        outs = (pl.BlockSpec(memory_space=pltpu.SMEM),) + outs[1:]
    return pl.pallas_call(
        kernel,
        out_shape=out,
        in_specs=specs,
        out_specs=outs,
        scratch_shapes=list(scratch),
        compiler_params=pltpu.CompilerParams(vmem_limit_bytes=limit << 20, flags=where.get("flags")),
        name=name,
    )(*inputs)


def body(visibilities, filters, counts, m_of_slot, band_of_block):
    struct = jax.ShapeDtypeStruct
    dma = pltpu.SemaphoreType.DMA
    group = ("grp", "core")
    spot = jnp.stack([lax.axis_index("grp"), lax.axis_index("core")])
    blocks = []
    for core, z in ORDER[:2]:
        to = (spot[0] + z) % 4 * 2 + (spot[1] + core) % 2
        blocks.append(lax.dynamic_index_in_dim(visibilities, to, 1, keepdims=False))
    sent = call(
        functools.partial(split_kernel, ORDER[2:]),
        "split",
        (struct((2, 64, 1024), BF16),) * 5,
        (spot, visibilities),
        [dma((10,))],
        smem=(0,),
        hbm=(1,),
        anyspace=(1,),
        out_any=True,
    )
    blocks += sent
    got = {}
    for (core, z), block in zip(ORDER, blocks):
        hop = [(k, (k // 2 + z) % 4 * 2 + (k + core) % 2) for k in range(8)]
        got[core, z] = lax.ppermute(block, group, hop)
    local = [got[hop] for hop in HOPS[1:]]

    rows = (m_of_slot % N2) * LANES + m_of_slot // N2
    to, own = call(
        invert_kernel,
        "invert",
        (struct((NT,), jnp.int32), struct((2, 64, 1024), BF16)),
        (spot, rows, visibilities),
        [dma((2,))],
        smem=(0, 1),
        hbm=(2,),
        anyspace=(2,),
        out_smem=True,
        limit=4,
    )
    tables = tuple(jnp.asarray(t) for t in twiddles())
    mid = pltpu.VMEM((4, 8, 2, 16, LANES), F32)
    same = call(
        early_kernel,
        "early",
        struct((N2, 64, 2 * LANES), BF16),
        (spot,) + tables + (own,) + tuple(local[:3]),
        [mid],
        smem=(0,),
    )
    spectrum = call(
        transform_kernel,
        "transform",
        struct((2 * NT, LANES), BF16),
        (spot, to, jnp.asarray(inner_matrix(), BF16)) + tables + (same,) + tuple(local[3:]),
        [
            mid,
            pltpu.VMEM((N2, 64, 2 * LANES), BF16),
            pltpu.VMEM((2 * LANES, LANES), F32),
            pltpu.VMEM((2 * LANES, LANES), F32),
            pltpu.VMEM((2 * NT, LANES), F32),
            pltpu.VMEM((2 * NT, LANES), BF16),
            dma((2 * NT // PIECE,)),
            pltpu.SMEM((NT + 1024,), jnp.int32),
            dma((1,)),
        ],
        smem=(0,),
        anyspace=(1,),
        out_any=True,
    )
    moved = lax.all_to_all(spectrum.reshape(DEVS, 2 * SLOTS, LANES), ALL, 0, 0, tiled=True)

    place = lax.axis_index(ALL).reshape(1)
    head, masked, col, hot = call(
        table_kernel,
        "tables",
        (
            struct((HEAD, 512), BF16),
            struct((4 * NB - HEAD, 512), BF16),
            struct((256, 128), jnp.int32), struct((128, 256), BF16)),
        (place, m_of_slot, counts, filters.reshape(SLOTS * KL, NB), band_of_block.T),
        [pltpu.VMEM((SLOTS * KL, NB), BF16), dma((4,))],
        smem=(0, 1, 2),
        anyspace=(3,),
        hbm=(3,),
    )
    kl, part = call(
        filter_kernel,
        "filter",
        (struct((512, KL), BF16), struct((DEVS, 128), F32)),
        (moved.reshape(4, 16, 2, 2 * SLOTS, LANES), head, masked, col, hot),
        [
            pltpu.VMEM((256, 128), F32),
            pltpu.VMEM((128, NB), BF16),
            pltpu.VMEM((4 * NB - HEAD, 512), BF16),
            dma((4,)),
        ],
        anyspace=(2,),
        hbm=(2,),
    )
    shares = lax.all_to_all(part[:, None, :], ALL, 0, 0, tiled=True)
    power = call(total_kernel, "total", struct((CH, 8), F32), (shares.reshape(DEVS, 128),), limit=4)
    return kl.reshape(SLOTS, 2, CH, KL), power


def solution(mesh):
    fine = Mesh(mesh.devices.reshape(4, 16, 2), ALL)
    wide = ("yx", "core")
    placed = (P(None, None, wide, "grp"), P(ALL, None, None), P(), P(), P())
    return jax.shard_map(
        body,
        mesh=fine,
        in_specs=placed,
        out_specs=(P(ALL, None, None, None), P(None, ALL)),
        check_vma=False,
    )
```
